32 devices in a mesh: fsdp: 32 (over z, y, x, core).
Axes of the slice: x: 2, y: 2, z: 4, core: 2. Of those that a mesh axis runs over, the one named last changes fastest.
Arguments:
- inputs: bfloat16 [16384, 576], P('fsdp'), may hold values from -6 to 6
- seq_lengths: int32 [32, 8], P('fsdp'), may hold values from 0 to 512, as said below
- w_query: bfloat16 [2, 331776], P(None, 'fsdp'), may hold values from -0.25 to 0.25
- w_key: bfloat16 [2, 110592], P(None, 'fsdp'), may hold values from -0.25 to 0.25
- w_value: bfloat16 [2, 110592], P(None, 'fsdp'), may hold values from -0.25 to 0.25
- w_out: bfloat16 [2, 331776], P(None, 'fsdp'), may hold values from -1.5 to 1.5
- w_gate: bfloat16 [2, 884736], P(None, 'fsdp'), may hold values from -0.25 to 0.25
- w_up: bfloat16 [2, 884736], P(None, 'fsdp'), may hold values from -0.25 to 0.25
- w_down: bfloat16 [2, 884736], P(None, 'fsdp'), may hold values from -0.15625 to 0.15625
- norm_gains: bfloat16 [2304], P('fsdp'), may hold values from 0.099609375 to 1.8984375
- cotangent: bfloat16 [16384, 576], P('fsdp'), may hold values from -6 to 6
Outputs:
- outputs: bfloat16 [16384, 576], P('fsdp')
- input_grad: bfloat16 [16384, 576], P('fsdp')
- grad_query: float32 [2, 331776], P(None, 'fsdp')
- grad_key: float32 [2, 110592], P(None, 'fsdp')
- grad_value: float32 [2, 110592], P(None, 'fsdp')
- grad_out: float32 [2, 331776], P(None, 'fsdp')
- grad_gate: float32 [2, 884736], P(None, 'fsdp')
- grad_up: float32 [2, 884736], P(None, 'fsdp')
- grad_down: float32 [2, 884736], P(None, 'fsdp')
- grad_gains: float32 [2304], P('fsdp')
The draws below stay inside these ranges and needn't reach their ends.
Inputs may be any that keep to these rules, and one draw needn't show every extreme that they name: `seq_lengths`: each device's row of 8 lengths sums to 512; a slot may be empty; in every draw some device holds a single sequence of 512 tokens.
All inputs are finite; a program needn't handle non-finite values.
Results may differ from the reference program's by a relative error of at most 0.023.
Values may be sent and summed in bfloat16 or wider, within the bound.
No kernel may reach another device: no remote copies, remote signals or barrier semaphores. Data moves between devices by JAX's collectives and lax.ppermute only.
A program may use at most 192 MiB of HBM per device.

```python
import math
import jax
import jax.numpy as jnp
from jax import lax

D = 576
H = 9
KVH = 3
HD = 64
FF = 1536
LAYERS = 2
SLOTS = 8
TOK_DEV = 512
KVW = 192
TOKENS = 16384
GAINS = 2304
N_FSDP = 32


def draw_seq_lengths(key, part):
    key_cut, key_keep, key_whole = jax.random.split(jax.random.fold_in(key, 11), 3)
    cuts = jax.random.randint(key_cut, (N_FSDP, SLOTS - 1), 0, TOK_DEV + 1).astype(jnp.int32)
    keep = jax.random.randint(key_keep, (N_FSDP, SLOTS - 1), 0, 2).astype(jnp.int32)
    whole = jax.random.randint(key_whole, (), 0, N_FSDP).astype(jnp.int32)
    device_rows = jnp.arange(N_FSDP, dtype=jnp.int32)[:, None]
    cuts = jnp.where(device_rows == whole, 0, cuts * keep).astype(jnp.int32)
    cuts = jnp.sort(cuts, axis=1)
    edges = jnp.concatenate([jnp.zeros((N_FSDP, 1), jnp.int32), cuts, jnp.full((N_FSDP, 1), TOK_DEV, jnp.int32)], axis=1)
    return (edges[:, 1:] - edges[:, :-1]).astype(jnp.int32)


def shard_levels(stream_key, extent, cuts, smallest, high):
    loudness, own = 1.0, jax.random.fold_in(stream_key, 6)
    for dim, shards_of in cuts:
        draws = jnp.exp(jax.random.uniform(jax.random.fold_in(own, dim), (shards_of,), jnp.float32, smallest / len(cuts), high / len(cuts)))
        loudness = loudness * jnp.repeat(draws, extent[dim] // shards_of).reshape([-1 if axis == dim else 1 for axis in range(len(extent))])
    return loudness


def normal_values(key, shape, deviation, most, cuts=(), held_as=jnp.bfloat16):
    drawn = deviation * jax.random.normal(key, shape, jnp.float32)
    if cuts:
        drawn = drawn * shard_levels(key, shape, cuts, -0.22, 0.18)
    return jnp.clip(drawn, -most, most).astype(held_as)


def setup_inputs(seed: int = 0) -> dict:
    seeds = jax.random.split(jax.random.key(seed), 12)
    return {
        "inputs": normal_values(seeds[0], (TOKENS, D), 1.0, 6.0, ((0, 32),)),
        "seq_lengths": draw_seq_lengths(jax.random.fold_in(seeds[11], 71), 0),
        "w_query": normal_values(seeds[2], (LAYERS, D * D), D ** -0.5, 0.25, ((1, 32),)),
        "w_key": normal_values(seeds[3], (LAYERS, D * KVW), D ** -0.5, 0.25, ((1, 32),)),
        "w_value": normal_values(seeds[4], (LAYERS, D * KVW), D ** -0.5, 0.25, ((1, 32),)),
        "w_out": normal_values(seeds[5], (LAYERS, D * D), (D // 32) ** -0.5, 1.5, ((1, 32),)),
        "w_gate": normal_values(seeds[6], (LAYERS, D * FF), D ** -0.5, 0.25, ((1, 32),)),
        "w_up": normal_values(seeds[7], (LAYERS, D * FF), D ** -0.5, 0.25, ((1, 32),)),
        "w_down": normal_values(seeds[8], (LAYERS, FF * D), FF ** -0.5, 0.15625, ((1, 32),)),
        "norm_gains": jnp.clip(1.0 + 0.18 * jax.random.normal(seeds[9], (GAINS,), jnp.float32), 0.099609375, 1.8984375).astype(jnp.bfloat16),
        "cotangent": normal_values(seeds[10], (TOKENS, D), 1.0, 6.0, ((0, 32),)),
    }


epsilon = 1e-05
rope_base = 100000.0
masked_score = -1e+30

@jax.custom_vjp
def low(v):
    return lax.optimization_barrier(v.astype(jnp.bfloat16)).astype(jnp.float32)

@jax.custom_vjp
def low_back(v):
    return v

def low_keep(v):
    return (low(v), None)

def low_pass(kept, grad):
    return (grad,)

def back_keep(v):
    return (v, None)

def back_low(kept, grad):
    return (low(grad),)
low.defvjp(low_keep, low_pass)
low_back.defvjp(back_keep, back_low)

def matmul(left, right):
    return jnp.dot(left, right, precision=lax.Precision.HIGHEST, preferred_element_type=jnp.float32)

def token_layout(seq_lengths):
    index = jnp.arange(TOK_DEV, dtype=jnp.int32)
    ends = jnp.cumsum(seq_lengths, axis=1).astype(jnp.int32)
    passed = index[None, :, None] >= ends[:, None, :]
    segment = lax.optimization_barrier(jnp.sum(passed.astype(jnp.int32), axis=2)).astype(jnp.int32)
    before = lax.optimization_barrier(jnp.sum(jnp.where(passed, seq_lengths[:, None, :], 0), axis=2)).astype(jnp.int32)
    position = (index[None, :] - before).astype(jnp.int32)
    return (segment, position)

def rope_tables(position):
    steps_half = jnp.arange(HD // 2, dtype=jnp.float32)
    freqs = jnp.exp(steps_half * (-2.0 * math.log(rope_base) / HD))
    angle = position.astype(jnp.float32)[..., None] * freqs
    cosine = jnp.concatenate([jnp.cos(angle), jnp.cos(angle)], axis=-1)
    sine_table = jnp.concatenate([jnp.sin(angle), jnp.sin(angle)], axis=-1)
    return (cosine, sine_table)

def rotate(values, cosine, sine_table):
    half = HD // 2
    turned = jnp.concatenate([-values[..., half:], values[..., :half]], axis=-1)
    return values * cosine + turned * sine_table

def rms_scale(state, gain):
    return state * lax.rsqrt(lax.optimization_barrier(jnp.mean(state * state, axis=-1, keepdims=True)) + epsilon) * gain

def attend_one(packed):
    queries, keys_all, values_all, segment = packed
    grouped = queries.reshape(TOK_DEV, KVH, H // KVH, HD)
    index = jnp.arange(TOK_DEV, dtype=jnp.int32)
    scores = jnp.einsum('qkgd,skd->kgqs', grouped, keys_all, precision=lax.Precision.HIGHEST) * (1.0 / math.sqrt(HD))
    scores = low_back(scores)
    allowed = (segment[:, None] == segment[None, :]) & (index[None, :] <= index[:, None])
    scores = jnp.where(allowed, scores, masked_score)
    largest = lax.optimization_barrier(jnp.max(scores, axis=-1, keepdims=True))
    weights = jnp.exp(scores - largest)
    probs = low(weights / lax.optimization_barrier(jnp.sum(weights, axis=-1, keepdims=True)))
    mixed = jnp.einsum('kgqs,skd->qkgd', probs, values_all, precision=lax.Precision.HIGHEST)
    return mixed.reshape(TOK_DEV, D)

def forward(inputs, w_query, w_key, w_value, w_out, w_gate, w_up, w_down, norm_gains, segment, cosine, sine_table):
    gains = norm_gains.reshape(LAYERS, 2, D)
    state = inputs
    for layer_index in range(LAYERS):
        normed = low(rms_scale(state, gains[layer_index, 0]))
        queries = rotate(low_back(matmul(normed, w_query[layer_index].reshape(D, D))).reshape(TOKENS, H, HD), cosine, sine_table)
        queries = low(queries)
        keys_all = rotate(low_back(matmul(normed, w_key[layer_index].reshape(D, KVW))).reshape(TOKENS, KVH, HD), cosine, sine_table)
        keys_all = low(keys_all)
        values_all = low(low_back(matmul(normed, w_value[layer_index].reshape(D, KVW)))).reshape(TOKENS, KVH, HD)
        attended = lax.map(jax.checkpoint(attend_one), (queries.reshape(N_FSDP, TOK_DEV, H, HD), keys_all.reshape(N_FSDP, TOK_DEV, KVH, HD), values_all.reshape(N_FSDP, TOK_DEV, KVH, HD), segment))
        attended = low(low_back(attended.reshape(TOKENS, D)))
        middle = state + low_back(matmul(attended, w_out[layer_index].reshape(D, D)))
        normed_ffn = low(rms_scale(middle, gains[layer_index, 1]))
        gate = low_back(matmul(normed_ffn, w_gate[layer_index].reshape(D, FF)))
        up_part = low_back(matmul(normed_ffn, w_up[layer_index].reshape(D, FF)))
        hidden = low(jax.nn.silu(gate) * up_part)
        state = middle + low_back(matmul(hidden, w_down[layer_index].reshape(FF, D)))
    return state

def reference(inputs, seq_lengths, w_query, w_key, w_value, w_out, w_gate, w_up, w_down, norm_gains, cotangent):
    segment, position = token_layout(seq_lengths)
    cosine, sine_table = rope_tables(position.reshape(TOKENS))
    cosine = cosine[:, None, :]
    sine_table = sine_table[:, None, :]
    floats = tuple((item.astype(jnp.float32) for item in (inputs, w_query, w_key, w_value, w_out, w_gate, w_up, w_down, norm_gains)))

    def apply_all(*params):
        return forward(*params, segment, cosine, sine_table)
    result, pullback = jax.vjp(apply_all, *floats)
    grads = pullback(cotangent.astype(jnp.float32))
    return (result.astype(jnp.bfloat16), grads[0].astype(jnp.bfloat16), grads[1], grads[2], grads[3], grads[4], grads[5], grads[6], grads[7], grads[8])
```

```python
import math

import jax
import jax.numpy as jnp
from jax import lax
from jax.sharding import PartitionSpec as P


D = 576
H = 9
KVH = 3
HD = 64
FF = 1536
LAYERS = 2
TOK_DEV = 512
QBLK = 512
KVW = 192


epsilon = 1e-05
rope_base = 100000.0
masked_score = -1e30


def product(left, right):
    return jnp.dot(left, right, preferred_element_type=jnp.float32)


def product_left(left, right):
    return lax.dot_general(
        left, right, (((0,), (0,)), ((), ())), preferred_element_type=jnp.float32
    )


def product_right(left, right):
    return lax.dot_general(
        left, right, (((1,), (1,)), ((), ())), preferred_element_type=jnp.float32
    )


def token_layout(lengths):
    index = jnp.arange(TOK_DEV, dtype=jnp.int32)
    ends = jnp.cumsum(lengths)
    passed = index[:, None] >= ends[None, :]
    segment = jnp.sum(passed.astype(jnp.int32), axis=1)
    position = index - jnp.sum(jnp.where(passed, lengths[None, :], 0), axis=1)
    steps_half = jnp.arange(HD // 2, dtype=jnp.float32)
    freqs = jnp.exp(steps_half * (-2.0 * math.log(rope_base) / HD))
    angle = position.astype(jnp.float32)[:, None] * freqs[None, :]
    cosine = jnp.concatenate([jnp.cos(angle), jnp.cos(angle)], axis=-1)[:, None, :]
    sine_table = jnp.concatenate([jnp.sin(angle), jnp.sin(angle)], axis=-1)[:, None, :]
    return (segment, cosine, sine_table)


def rotate(values, cosine, sine_table):
    half = HD // 2
    turned = jnp.concatenate([-values[..., half:], values[..., :half]], axis=-1)
    return values * cosine + turned * sine_table


def rotate_back(grads, cosine, sine_table):
    half = HD // 2
    shifted = grads * sine_table
    turned = jnp.concatenate([shifted[..., half:], -shifted[..., :half]], axis=-1)
    return grads * cosine + turned


def block_scores(grouped_rows, keys_part, segment, first, last):
    index = jnp.arange(last, dtype=jnp.int32)
    allowed = (segment[first:last, None] == segment[None, :last]) & (
        index[None, :] <= index[first:last, None]
    )
    scores = jnp.einsum(
        "qkgd,skd->kgqs", grouped_rows, keys_part, preferred_element_type=jnp.float32
    ) * (1.0 / math.sqrt(HD))
    return jnp.where(allowed, scores, masked_score)


def attend(queries, keys_all, values_all, segment):
    grouped = queries.reshape(TOK_DEV, KVH, H // KVH, HD)
    last = QBLK
    scores = block_scores(grouped, keys_all, segment, 0, last)
    largest = jnp.max(scores, axis=-1, keepdims=True)
    weights = jnp.exp(scores - largest)
    weight_sum = jnp.sum(weights, axis=-1, keepdims=True)
    probs = (weights / weight_sum).astype(jnp.bfloat16)
    mixed = jnp.einsum("kgqs,skd->qkgd", probs, values_all, preferred_element_type=jnp.float32)
    results = mixed.reshape(QBLK, D)
    totals = [largest + jnp.log(weight_sum)]
    return (results, totals)


def attend_back(queries, keys_all, values_all, segment, totals, grad_mixed):
    grouped = queries.reshape(TOK_DEV, KVH, H // KVH, HD)
    grad_grouped = grad_mixed.reshape(TOK_DEV, KVH, H // KVH, HD)
    grad_keys = jnp.zeros((TOK_DEV, KVH, HD), jnp.float32)
    grad_values = jnp.zeros((TOK_DEV, KVH, HD), jnp.float32)
    scale = 1.0 / math.sqrt(HD)
    last = QBLK
    scores = block_scores(grouped, keys_all, segment, 0, last)
    probs = jnp.exp(scores - totals[0])
    probs_low = probs.astype(jnp.bfloat16)
    grad_values = grad_values.at[:last].add(
        jnp.einsum("kgqs,qkgd->skd", probs_low, grad_grouped, preferred_element_type=jnp.float32)
    )
    grad_probs = jnp.einsum(
        "qkgd,skd->kgqs", grad_grouped, values_all, preferred_element_type=jnp.float32
    )
    inner = jnp.sum(probs * grad_probs, axis=-1, keepdims=True)
    grad_scores = (probs * (grad_probs - inner)).astype(jnp.bfloat16)
    grad_queries = (
        jnp.einsum("kgqs,skd->qkgd", grad_scores, keys_all, preferred_element_type=jnp.float32)
        * scale
    )
    grad_keys = grad_keys.at[:last].add(
        jnp.einsum("kgqs,qkgd->skd", grad_scores, grouped, preferred_element_type=jnp.float32)
        * scale
    )
    grad_query_all = grad_queries.reshape(TOK_DEV, H, HD)
    return (grad_query_all, grad_keys, grad_values)


def norm_back(grad_normed, source, inverse_rms, gain):
    scaled = grad_normed * gain
    grad_gain = jnp.sum(grad_normed * source * inverse_rms, axis=0)
    grad_source = (
        inverse_rms * scaled
        - inverse_rms
        * inverse_rms
        * inverse_rms
        * source
        * jnp.mean(scaled * source, axis=-1, keepdims=True)
    )
    return (grad_source, grad_gain)


def flat_shards(shards):
    return tuple((member.reshape(-1) for member in shards))


def unpack(whole, layer_index, devices):
    shapes = ((D, D), (D, KVW), (D, KVW), (D, D), (D, FF), (D, FF), (FF, D))
    result = []
    for member_index in range(7):
        laid = whole[member_index].reshape(devices, -1)
        width = laid.shape[1] // LAYERS
        result.append(
            laid[:, layer_index * width : (layer_index + 1) * width].reshape(shapes[member_index])
        )
    return tuple(result)


def layer_forward(state, weights, gain_pair, segment, cosine, sine_table):
    w_q, w_k, w_v, w_o, w_g, w_u, w_d = weights
    rms_attn = lax.rsqrt(jnp.mean(state * state, axis=-1, keepdims=True) + epsilon)
    normed_attn = (state * rms_attn * gain_pair[0]).astype(jnp.bfloat16)
    queries = rotate(product(normed_attn, w_q).reshape(TOK_DEV, H, HD), cosine, sine_table).astype(
        jnp.bfloat16
    )
    keys_all = rotate(
        product(normed_attn, w_k).reshape(TOK_DEV, KVH, HD), cosine, sine_table
    ).astype(jnp.bfloat16)
    values_all = product(normed_attn, w_v).astype(jnp.bfloat16).reshape(TOK_DEV, KVH, HD)
    mixed, totals = attend(queries, keys_all, values_all, segment)
    attended = mixed.astype(jnp.bfloat16)
    middle = state + product(attended, w_o)
    rms_ffn = lax.rsqrt(jnp.mean(middle * middle, axis=-1, keepdims=True) + epsilon)
    normed_ffn = (middle * rms_ffn * gain_pair[1]).astype(jnp.bfloat16)
    gate = product(normed_ffn, w_g)
    up_part = product(normed_ffn, w_u)
    hidden = (jax.nn.silu(gate) * up_part).astype(jnp.bfloat16)
    result = middle + product(hidden, w_d)
    saved = (
        state,
        rms_attn,
        normed_attn,
        queries,
        keys_all,
        values_all,
        totals,
        attended,
        middle,
        rms_ffn,
        normed_ffn,
        gate,
        up_part,
        hidden,
    )
    return (result, saved)


def layer_backward(grad_result, saved, weights, gain_pair, segment, cosine, sine_table):
    w_q, w_k, w_v, w_o, w_g, w_u, w_d = weights
    (
        state,
        rms_attn,
        normed_attn,
        queries,
        keys_all,
        values_all,
        totals,
        attended,
        middle,
        rms_ffn,
        normed_ffn,
        gate,
        up_part,
        hidden,
    ) = saved
    grad_branch = grad_result.astype(jnp.bfloat16)
    grad_wd = product_left(hidden, grad_branch)
    grad_hidden = product_right(grad_branch, w_d)
    sigmoid_gate = jax.nn.sigmoid(gate)
    grad_gate = (grad_hidden * up_part * sigmoid_gate * (1.0 + gate * (1.0 - sigmoid_gate))).astype(
        jnp.bfloat16
    )
    grad_upper = (grad_hidden * gate * sigmoid_gate).astype(jnp.bfloat16)
    grad_wg = product_left(normed_ffn, grad_gate)
    grad_wu = product_left(normed_ffn, grad_upper)
    grad_normed_ffn = product_right(grad_gate, w_g) + product_right(grad_upper, w_u)
    grad_mid_norm, grad_gain_ffn = norm_back(grad_normed_ffn, middle, rms_ffn, gain_pair[1])
    grad_middle = grad_result + grad_mid_norm
    grad_attn_branch = grad_middle.astype(jnp.bfloat16)
    grad_wo = product_left(attended, grad_attn_branch)
    grad_mixed = product_right(grad_attn_branch, w_o).astype(jnp.bfloat16)
    grad_queries, grad_keys, grad_values = attend_back(
        queries, keys_all, values_all, segment, totals, grad_mixed
    )
    grad_queries = (
        rotate_back(grad_queries, cosine, sine_table).reshape(TOK_DEV, D).astype(jnp.bfloat16)
    )
    grad_keys = (
        rotate_back(grad_keys, cosine, sine_table).reshape(TOK_DEV, KVW).astype(jnp.bfloat16)
    )
    grad_values = grad_values.reshape(TOK_DEV, KVW).astype(jnp.bfloat16)
    grad_wq = product_left(normed_attn, grad_queries)
    grad_wk = product_left(normed_attn, grad_keys)
    grad_wv = product_left(normed_attn, grad_values)
    grad_normed_attn = (
        product_right(grad_queries, w_q)
        + product_right(grad_keys, w_k)
        + product_right(grad_values, w_v)
    )
    grad_state_norm, grad_gain_attn = norm_back(grad_normed_attn, state, rms_attn, gain_pair[0])
    grad_state = grad_middle + grad_state_norm
    return (
        grad_state,
        (grad_wq, grad_wk, grad_wv, grad_wo, grad_wg, grad_wu, grad_wd),
        jnp.stack([grad_gain_attn, grad_gain_ffn]),
    )


def per_device(
    inputs, seq_lengths, w_query, w_key, w_value, w_out, w_gate, w_up, w_down, norm_gains, cotangent
):
    devices = lax.axis_size("fsdp")
    segment, cosine, sine_table = token_layout(seq_lengths[0])
    flat = flat_shards((w_query, w_key, w_value, w_out, w_gate, w_up, w_down))
    whole = (
        lax.all_gather(flat[0], "fsdp", axis=0, tiled=True),
        lax.all_gather(flat[1], "fsdp", axis=0, tiled=True),
        lax.all_gather(flat[2], "fsdp", axis=0, tiled=True),
        lax.all_gather(flat[3], "fsdp", axis=0, tiled=True),
        lax.all_gather(flat[4], "fsdp", axis=0, tiled=True),
        lax.all_gather(flat[5], "fsdp", axis=0, tiled=True),
        lax.all_gather(flat[6], "fsdp", axis=0, tiled=True),
        lax.all_gather(norm_gains, "fsdp", axis=0, tiled=True),
    )
    weights = [unpack(whole, layer_index, devices) for layer_index in range(LAYERS)]
    gains = whole[7].reshape(LAYERS, 2, D).astype(jnp.float32)
    state = inputs.astype(jnp.float32)
    saved = []
    for layer_index in range(LAYERS):
        state, kept_layer = layer_forward(
            state, weights[layer_index], gains[layer_index], segment, cosine, sine_table
        )
        saved.append(kept_layer)
    outputs = state.astype(jnp.bfloat16)
    whole = (
        lax.all_gather(flat[0], "fsdp", axis=0, tiled=True),
        lax.all_gather(flat[1], "fsdp", axis=0, tiled=True),
        lax.all_gather(flat[2], "fsdp", axis=0, tiled=True),
        lax.all_gather(flat[3], "fsdp", axis=0, tiled=True),
        lax.all_gather(flat[4], "fsdp", axis=0, tiled=True),
        lax.all_gather(flat[5], "fsdp", axis=0, tiled=True),
        lax.all_gather(flat[6], "fsdp", axis=0, tiled=True),
        lax.all_gather(norm_gains, "fsdp", axis=0, tiled=True),
    )
    weights = [unpack(whole, layer_index, devices) for layer_index in range(LAYERS)]
    gains = whole[7].reshape(LAYERS, 2, D).astype(jnp.float32)
    grad_state = cotangent.astype(jnp.float32)
    layer_grads = [None] * LAYERS
    gain_grads = [None] * LAYERS
    shard_grads = [None] * LAYERS
    gain_result = None
    for layer_index in reversed(range(LAYERS)):
        grad_state, layer_grads[layer_index], gain_grads[layer_index] = layer_backward(
            grad_state,
            saved[layer_index],
            weights[layer_index],
            gains[layer_index],
            segment,
            cosine,
            sine_table,
        )
        grad_q, grad_k, grad_v, grad_o, grad_g, grad_u, grad_d = [
            member.reshape(-1) for member in layer_grads[layer_index]
        ]
        if layer_index > 0:
            shard_grads[layer_index] = (
                lax.psum_scatter(grad_q, "fsdp", scatter_dimension=0, tiled=True),
                lax.psum_scatter(grad_k, "fsdp", scatter_dimension=0, tiled=True),
                lax.psum_scatter(grad_v, "fsdp", scatter_dimension=0, tiled=True),
                lax.psum_scatter(grad_o, "fsdp", scatter_dimension=0, tiled=True),
                lax.psum_scatter(grad_g, "fsdp", scatter_dimension=0, tiled=True),
                lax.psum_scatter(grad_u, "fsdp", scatter_dimension=0, tiled=True),
                lax.psum_scatter(grad_d, "fsdp", scatter_dimension=0, tiled=True),
            )
        else:
            gain_total = jnp.stack(gain_grads).reshape(-1)
            summed = (
                lax.psum_scatter(grad_q, "fsdp", scatter_dimension=0, tiled=True),
                lax.psum_scatter(grad_k, "fsdp", scatter_dimension=0, tiled=True),
                lax.psum_scatter(grad_v, "fsdp", scatter_dimension=0, tiled=True),
                lax.psum_scatter(grad_o, "fsdp", scatter_dimension=0, tiled=True),
                lax.psum_scatter(grad_g, "fsdp", scatter_dimension=0, tiled=True),
                lax.psum_scatter(grad_u, "fsdp", scatter_dimension=0, tiled=True),
                lax.psum_scatter(grad_d, "fsdp", scatter_dimension=0, tiled=True),
                lax.psum_scatter(gain_total, "fsdp", scatter_dimension=0, tiled=True),
            )
            shard_grads[0] = summed[:7]
            gain_result = summed[7]
    final = [
        jnp.stack([shard_grads[layer_index][member_index] for layer_index in range(LAYERS)], axis=0)
        for member_index in range(7)
    ]
    return (
        outputs,
        grad_state.astype(jnp.bfloat16),
        final[0],
        final[1],
        final[2],
        final[3],
        final[4],
        final[5],
        final[6],
        gain_result,
    )

def fast_sizes(devices):
    if devices & (devices - 1) or D % devices or FF % devices:
        return None
    rows = D // devices
    pad = -(-rows // 8) * 8
    if (FF // devices) % pad:
        return None
    return (rows, pad, FF // devices // pad)


def exchange(value, bit, devices):
    return lax.ppermute(value, "fsdp", [(i, i ^ bit) for i in range(devices)])


def gather_slab(slab, order, bits, devices):
    rows, width = slab.shape
    held = slab.reshape((1,) * len(bits) + (rows, width))
    for bit in order:
        held = jnp.concatenate([held, exchange(held, bit, devices)], axis=bits.index(bit))
    return held.reshape(devices * rows, width)


def scatter_slab(parts, order, bits, devices):
    rows = parts.shape[0] // devices
    held = parts.reshape((2,) * len(bits) + (rows, parts.shape[1]))
    for bit in reversed(order):
        axis = bits.index(bit)
        keep = lax.slice_in_dim(held, 0, 1, axis=axis)
        send = lax.slice_in_dim(held, 1, 2, axis=axis)
        total = keep.astype(jnp.float32) + exchange(send, bit, devices).astype(jnp.float32)
        held = total if bit == order[0] else total.astype(jnp.bfloat16)
    return held.reshape(rows, parts.shape[1])


def fast_device(
    inputs, seq_lengths, w_query, w_key, w_value, w_out, w_gate, w_up, w_down, norm_gains, cotangent
):
    devices = lax.axis_size("fsdp")
    rows, pad, folds = fast_sizes(devices)
    low = jnp.bfloat16
    segment, cosine, sine_table = token_layout(seq_lengths[0])
    me = lax.axis_index("fsdp")

    count = devices.bit_length() - 1
    bits = [1] + [1 << i for i in range(count - 1, 0, -1)]
    rest = bits[1:]
    first, others = rest[:1], rest[1:]

    def turned(shift):
        shift = shift % max(len(others), 1)
        return first + others[shift:] + others[:shift] + [1]

    orders = (turned(1), turned(2), turned(0))
    orders = tuple([o[:1] + o[1:-1][::-1] + o[-1:] for o in orders])

    block = jnp.arange(devices, dtype=jnp.int32)
    half = devices // 2
    owner = me ^ (((block % half) << 1) | (block // half))
    other = me ^ block
    place = (other >> 1) + (other & 1) * half

    column = jnp.arange(devices * pad, dtype=jnp.int32)
    inside = column % pad
    feature = jnp.where(inside < rows, jnp.repeat(owner, pad) * rows + inside, -1)
    spread = (jnp.arange(D, dtype=jnp.int32)[:, None] == feature[None, :]).astype(low)

    def spread_out(value):
        return jnp.dot(value, spread, preferred_element_type=jnp.float32).astype(low)

    def bring_back(value):
        return product_right(value.astype(low), spread)

    def packed(layer):
        def cut(member, width):
            return member[layer].reshape(rows, width)

        folded = w_down[layer].reshape(folds, pad, D)

        def padded(members, extra):
            body = jnp.concatenate(members, axis=1)
            body = jnp.pad(body, ((0, pad - rows), (0, 0)))
            if extra:
                body = jnp.concatenate([body] + extra, axis=1)
            return body

        even = [folded[i] for i in range(0, folds, 2)]
        odd = [folded[i] for i in range(1, folds, 2)]
        attn = padded([cut(w_query, D), cut(w_key, KVW), cut(w_value, KVW), cut(w_out, D)], even)
        if layer == 0:
            share = norm_gains.shape[0]
            attn = attn + jnp.pad(
                norm_gains[None, :], ((rows, pad - rows - 1), (0, attn.shape[1] - share))
            )
        return (attn, padded([cut(w_gate, FF)], odd), padded([cut(w_up, FF)], []))

    slabs = [packed(layer) for layer in range(LAYERS)]
    whole = []
    for layer in range(LAYERS):
        whole.append(
            [gather_slab(slabs[layer][i], orders[i], bits, devices) for i in range(3)]
        )
    share = norm_gains.shape[0]
    gains = jnp.take(whole[0][0].reshape(devices, pad, -1)[:, rows, :share], place, axis=0)
    gains = gains.reshape(LAYERS, 2, D).astype(jnp.float32)

    ends = (D, D + KVW, D + 2 * KVW, 2 * D + 2 * KVW)

    def unpacked(parts):
        attn, gate, up_part = parts
        evens = attn[:, ends[3] :].reshape(devices, pad, -1, D)
        odds = gate[:, FF:].reshape(devices, pad, -1, D)
        pieces = [(evens if i % 2 == 0 else odds)[:, :, i // 2] for i in range(folds)]
        down = jnp.take(jnp.stack(pieces, axis=1), place, axis=0).reshape(FF, D)
        return (attn[:, : ends[2]], attn[:, ends[2] : ends[3]], gate[:, :FF], up_part, down)

    weights = [unpacked(whole[layer]) for layer in range(LAYERS)]

    def forward(state, layer):
        w_qkv, w_o, w_g, w_u, w_d = weights[layer]
        gain_pair = gains[layer]
        rms_attn = lax.rsqrt(jnp.mean(state * state, axis=-1, keepdims=True) + epsilon)
        normed_attn = spread_out((state * rms_attn * gain_pair[0]).astype(low))
        qkv = product(normed_attn, w_qkv)
        queries = rotate(qkv[:, :D].reshape(TOK_DEV, H, HD), cosine, sine_table).astype(low)
        keys_all = rotate(
            qkv[:, D : D + KVW].reshape(TOK_DEV, KVH, HD), cosine, sine_table
        ).astype(low)
        values_all = qkv[:, D + KVW :].astype(low).reshape(TOK_DEV, KVH, HD)
        mixed, totals = attend(queries, keys_all, values_all, segment)
        attended = spread_out(mixed.astype(low))
        middle = state + product(attended, w_o)
        rms_ffn = lax.rsqrt(jnp.mean(middle * middle, axis=-1, keepdims=True) + epsilon)
        normed_ffn = spread_out((middle * rms_ffn * gain_pair[1]).astype(low))
        gate = product(normed_ffn, w_g)
        up_part = product(normed_ffn, w_u)
        hidden = (jax.nn.silu(gate) * up_part).astype(low)
        result = middle + product(hidden, w_d)
        saved = (
            state,
            rms_attn,
            normed_attn,
            queries,
            keys_all,
            values_all,
            totals,
            attended,
            middle,
            rms_ffn,
            normed_ffn,
            gate,
            up_part,
            hidden,
        )
        return (result, saved)

    def backward(grad_result, saved, layer):
        w_qkv, w_o, w_g, w_u, w_d = weights[layer]
        gain_pair = gains[layer]
        (
            state,
            rms_attn,
            normed_attn,
            queries,
            keys_all,
            values_all,
            totals,
            attended,
            middle,
            rms_ffn,
            normed_ffn,
            gate,
            up_part,
            hidden,
        ) = saved
        grad_branch = grad_result.astype(low)
        grad_wd = product_left(hidden, grad_branch).astype(low)
        grad_wd = jnp.take(grad_wd.reshape(devices, folds, pad, D), owner, axis=0)
        grad_hidden = product_right(grad_branch, w_d)
        sigmoid_gate = jax.nn.sigmoid(gate)
        grad_gate = (
            grad_hidden * up_part * sigmoid_gate * (1.0 + gate * (1.0 - sigmoid_gate))
        ).astype(low)
        grad_upper = (grad_hidden * gate * sigmoid_gate).astype(low)
        grad_wg = product_left(normed_ffn, grad_gate).astype(low)
        grad_wu = product_left(normed_ffn, grad_upper).astype(low)

        def folded(start):
            return [grad_wd[:, i].reshape(devices * pad, D) for i in range(start, folds, 2)]

        shard_u = scatter_slab(grad_wu, orders[2], bits, devices)
        shard_g = scatter_slab(
            jnp.concatenate([grad_wg] + folded(1), axis=1), orders[1], bits, devices
        )
        grad_normed_ffn = bring_back(product_right(grad_gate, w_g) + product_right(grad_upper, w_u))
        grad_mid_norm, grad_gain_ffn = norm_back(grad_normed_ffn, middle, rms_ffn, gain_pair[1])
        grad_middle = grad_result + grad_mid_norm
        grad_attn_branch = grad_middle.astype(low)
        grad_wo = product_left(attended, grad_attn_branch).astype(low)
        grad_mixed = bring_back(product_right(grad_attn_branch, w_o)).astype(low)
        grad_queries, grad_keys, grad_values = attend_back(
            queries, keys_all, values_all, segment, totals, grad_mixed
        )
        grad_queries = rotate_back(grad_queries, cosine, sine_table).reshape(TOK_DEV, D)
        grad_keys = rotate_back(grad_keys, cosine, sine_table).reshape(TOK_DEV, KVW)
        grad_values = grad_values.reshape(TOK_DEV, KVW)
        grad_qkv = jnp.concatenate([grad_queries, grad_keys, grad_values], axis=1).astype(low)
        grad_wqkv = product_left(normed_attn, grad_qkv).astype(low)
        grad_normed_attn = bring_back(product_right(grad_qkv, w_qkv))
        grad_state_norm, grad_gain_attn = norm_back(grad_normed_attn, state, rms_attn, gain_pair[0])
        grad_state = grad_middle + grad_state_norm
        attn = jnp.concatenate([grad_wqkv, grad_wo] + folded(0), axis=1)
        return (grad_state, attn, shard_g, shard_u, jnp.stack([grad_gain_attn, grad_gain_ffn]))

    state = inputs.astype(jnp.float32)
    kept = []
    for layer in range(LAYERS):
        state, saved = forward(state, layer)
        kept.append(saved)
    outputs = state.astype(low)
    grad_state = cotangent.astype(jnp.float32)
    shards = [None] * LAYERS
    gain_grads = [None] * LAYERS
    for layer in reversed(range(LAYERS)):
        grad_state, attn, shard_g, shard_u, gain_grads[layer] = backward(
            grad_state, kept[layer], layer
        )
        if layer == 0:
            total = jnp.stack(gain_grads).reshape(devices, share)
            total = jnp.take(total, owner, axis=0).astype(low)
            total = jnp.pad(
                total[:, None, :], ((0, 0), (rows, pad - rows - 1), (0, attn.shape[1] - share))
            )
            attn = attn + total.reshape(attn.shape)
        shards[layer] = (scatter_slab(attn, orders[0], bits, devices), shard_g, shard_u)

    gain_result = shards[0][0][rows, :share]
    results = []
    bounds = (0,) + ends
    for index in range(4):
        results.append([part[0][:rows, bounds[index] : bounds[index + 1]] for part in shards])
    results.append([part[1][:rows, :FF] for part in shards])
    results.append([part[2][:rows] for part in shards])
    downs = []
    for attn, gate, _ in shards:
        evens = attn[:, ends[3] :].reshape(pad, -1, D)
        odds = gate[:, FF:].reshape(pad, -1, D)
        downs.append(
            jnp.stack([(evens if i % 2 == 0 else odds)[:, i // 2] for i in range(folds)], axis=0)
        )
    results.append(downs)
    final = [jnp.stack([member.reshape(-1) for member in pair], axis=0) for pair in results]
    return (
        outputs,
        grad_state.astype(low),
        final[0],
        final[1],
        final[2],
        final[3],
        final[4],
        final[5],
        final[6],
        gain_result,
    )


def solution(mesh):
    placed = (
        P("fsdp", None),
        P("fsdp", None),
        P(None, "fsdp"),
        P(None, "fsdp"),
        P(None, "fsdp"),
        P(None, "fsdp"),
        P(None, "fsdp"),
        P(None, "fsdp"),
        P(None, "fsdp"),
        P("fsdp"),
        P("fsdp", None),
    )
    body = per_device if fast_sizes(mesh.shape["fsdp"]) is None else fast_device
    return jax.shard_map(
        body,
        mesh=mesh,
        in_specs=placed,
        out_specs=(
            P("fsdp", None),
            P("fsdp", None),
            P(None, "fsdp"),
            P(None, "fsdp"),
            P(None, "fsdp"),
            P(None, "fsdp"),
            P(None, "fsdp"),
            P(None, "fsdp"),
            P(None, "fsdp"),
            P("fsdp"),
        ),
        check_vma=False,
    )
```

```python
import math

import jax
import jax.numpy as jnp
from jax import lax
from jax.experimental import pallas as pl
from jax.experimental.pallas import tpu as pltpu
from jax.sharding import PartitionSpec as P


D = 576
H = 9
KVH = 3
HD = 64
FF = 1536
LAYERS = 2
TOK_DEV = 512
QBLK = 512
KVW = 192


epsilon = 1e-05
rope_base = 100000.0
masked_score = -1e30


def product(left, right):
    return jnp.dot(left, right, preferred_element_type=jnp.float32)


def product_left(left, right):
    return lax.dot_general(
        left, right, (((0,), (0,)), ((), ())), preferred_element_type=jnp.float32
    )


def product_right(left, right):
    return lax.dot_general(
        left, right, (((1,), (1,)), ((), ())), preferred_element_type=jnp.float32
    )


def token_layout(lengths):
    index = jnp.arange(TOK_DEV, dtype=jnp.int32)
    ends = jnp.cumsum(lengths)
    passed = index[:, None] >= ends[None, :]
    segment = jnp.sum(passed.astype(jnp.int32), axis=1)
    position = index - jnp.sum(jnp.where(passed, lengths[None, :], 0), axis=1)
    steps_half = jnp.arange(HD // 2, dtype=jnp.float32)
    freqs = jnp.exp(steps_half * (-2.0 * math.log(rope_base) / HD))
    angle = position.astype(jnp.float32)[:, None] * freqs[None, :]
    cosine = jnp.concatenate([jnp.cos(angle), jnp.cos(angle)], axis=-1)[:, None, :]
    sine_table = jnp.concatenate([jnp.sin(angle), jnp.sin(angle)], axis=-1)[:, None, :]
    return (segment, cosine, sine_table)


def rotate(values, cosine, sine_table):
    half = HD // 2
    turned = jnp.concatenate([-values[..., half:], values[..., :half]], axis=-1)
    return values * cosine + turned * sine_table


def rotate_back(grads, cosine, sine_table):
    half = HD // 2
    shifted = grads * sine_table
    turned = jnp.concatenate([shifted[..., half:], -shifted[..., :half]], axis=-1)
    return grads * cosine + turned


def block_scores(grouped_rows, keys_part, segment, first, last):
    index = jnp.arange(last, dtype=jnp.int32)
    allowed = (segment[first:last, None] == segment[None, :last]) & (
        index[None, :] <= index[first:last, None]
    )
    scores = jnp.einsum(
        "qkgd,skd->kgqs", grouped_rows, keys_part, preferred_element_type=jnp.float32
    ) * (1.0 / math.sqrt(HD))
    return jnp.where(allowed, scores, masked_score)


def attend(queries, keys_all, values_all, segment):
    grouped = queries.reshape(TOK_DEV, KVH, H // KVH, HD)
    last = QBLK
    scores = block_scores(grouped, keys_all, segment, 0, last)
    largest = jnp.max(scores, axis=-1, keepdims=True)
    weights = jnp.exp(scores - largest)
    weight_sum = jnp.sum(weights, axis=-1, keepdims=True)
    probs = (weights / weight_sum).astype(jnp.bfloat16)
    mixed = jnp.einsum("kgqs,skd->qkgd", probs, values_all, preferred_element_type=jnp.float32)
    results = mixed.reshape(QBLK, D)
    totals = [largest + jnp.log(weight_sum)]
    return (results, totals)


def attend_back(queries, keys_all, values_all, segment, totals, grad_mixed):
    grouped = queries.reshape(TOK_DEV, KVH, H // KVH, HD)
    grad_grouped = grad_mixed.reshape(TOK_DEV, KVH, H // KVH, HD)
    grad_keys = jnp.zeros((TOK_DEV, KVH, HD), jnp.float32)
    grad_values = jnp.zeros((TOK_DEV, KVH, HD), jnp.float32)
    scale = 1.0 / math.sqrt(HD)
    last = QBLK
    scores = block_scores(grouped, keys_all, segment, 0, last)
    probs = jnp.exp(scores - totals[0])
    probs_low = probs.astype(jnp.bfloat16)
    grad_values = grad_values.at[:last].add(
        jnp.einsum("kgqs,qkgd->skd", probs_low, grad_grouped, preferred_element_type=jnp.float32)
    )
    grad_probs = jnp.einsum(
        "qkgd,skd->kgqs", grad_grouped, values_all, preferred_element_type=jnp.float32
    )
    inner = jnp.sum(probs * grad_probs, axis=-1, keepdims=True)
    grad_scores = (probs * (grad_probs - inner)).astype(jnp.bfloat16)
    grad_queries = (
        jnp.einsum("kgqs,skd->qkgd", grad_scores, keys_all, preferred_element_type=jnp.float32)
        * scale
    )
    grad_keys = grad_keys.at[:last].add(
        jnp.einsum("kgqs,qkgd->skd", grad_scores, grouped, preferred_element_type=jnp.float32)
        * scale
    )
    grad_query_all = grad_queries.reshape(TOK_DEV, H, HD)
    return (grad_query_all, grad_keys, grad_values)


def norm_back(grad_normed, source, inverse_rms, gain):
    scaled = grad_normed * gain
    grad_gain = jnp.sum(grad_normed * source * inverse_rms, axis=0)
    grad_source = (
        inverse_rms * scaled
        - inverse_rms
        * inverse_rms
        * inverse_rms
        * source
        * jnp.mean(scaled * source, axis=-1, keepdims=True)
    )
    return (grad_source, grad_gain)


def flat_shards(shards):
    return tuple((member.reshape(-1) for member in shards))


def unpack(whole, layer_index, devices):
    shapes = ((D, D), (D, KVW), (D, KVW), (D, D), (D, FF), (D, FF), (FF, D))
    result = []
    for member_index in range(7):
        laid = whole[member_index].reshape(devices, -1)
        width = laid.shape[1] // LAYERS
        result.append(
            laid[:, layer_index * width : (layer_index + 1) * width].reshape(shapes[member_index])
        )
    return tuple(result)


def layer_forward(state, weights, gain_pair, segment, cosine, sine_table):
    w_q, w_k, w_v, w_o, w_g, w_u, w_d = weights
    rms_attn = lax.rsqrt(jnp.mean(state * state, axis=-1, keepdims=True) + epsilon)
    normed_attn = (state * rms_attn * gain_pair[0]).astype(jnp.bfloat16)
    queries = rotate(product(normed_attn, w_q).reshape(TOK_DEV, H, HD), cosine, sine_table).astype(
        jnp.bfloat16
    )
    keys_all = rotate(
        product(normed_attn, w_k).reshape(TOK_DEV, KVH, HD), cosine, sine_table
    ).astype(jnp.bfloat16)
    values_all = product(normed_attn, w_v).astype(jnp.bfloat16).reshape(TOK_DEV, KVH, HD)
    mixed, totals = attend(queries, keys_all, values_all, segment)
    attended = mixed.astype(jnp.bfloat16)
    middle = state + product(attended, w_o)
    rms_ffn = lax.rsqrt(jnp.mean(middle * middle, axis=-1, keepdims=True) + epsilon)
    normed_ffn = (middle * rms_ffn * gain_pair[1]).astype(jnp.bfloat16)
    gate = product(normed_ffn, w_g)
    up_part = product(normed_ffn, w_u)
    hidden = (jax.nn.silu(gate) * up_part).astype(jnp.bfloat16)
    result = middle + product(hidden, w_d)
    saved = (
        state,
        rms_attn,
        normed_attn,
        queries,
        keys_all,
        values_all,
        totals,
        attended,
        middle,
        rms_ffn,
        normed_ffn,
        gate,
        up_part,
        hidden,
    )
    return (result, saved)


def layer_backward(grad_result, saved, weights, gain_pair, segment, cosine, sine_table):
    w_q, w_k, w_v, w_o, w_g, w_u, w_d = weights
    (
        state,
        rms_attn,
        normed_attn,
        queries,
        keys_all,
        values_all,
        totals,
        attended,
        middle,
        rms_ffn,
        normed_ffn,
        gate,
        up_part,
        hidden,
    ) = saved
    grad_branch = grad_result.astype(jnp.bfloat16)
    grad_wd = product_left(hidden, grad_branch)
    grad_hidden = product_right(grad_branch, w_d)
    sigmoid_gate = jax.nn.sigmoid(gate)
    grad_gate = (grad_hidden * up_part * sigmoid_gate * (1.0 + gate * (1.0 - sigmoid_gate))).astype(
        jnp.bfloat16
    )
    grad_upper = (grad_hidden * gate * sigmoid_gate).astype(jnp.bfloat16)
    grad_wg = product_left(normed_ffn, grad_gate)
    grad_wu = product_left(normed_ffn, grad_upper)
    grad_normed_ffn = product_right(grad_gate, w_g) + product_right(grad_upper, w_u)
    grad_mid_norm, grad_gain_ffn = norm_back(grad_normed_ffn, middle, rms_ffn, gain_pair[1])
    grad_middle = grad_result + grad_mid_norm
    grad_attn_branch = grad_middle.astype(jnp.bfloat16)
    grad_wo = product_left(attended, grad_attn_branch)
    grad_mixed = product_right(grad_attn_branch, w_o).astype(jnp.bfloat16)
    grad_queries, grad_keys, grad_values = attend_back(
        queries, keys_all, values_all, segment, totals, grad_mixed
    )
    grad_queries = (
        rotate_back(grad_queries, cosine, sine_table).reshape(TOK_DEV, D).astype(jnp.bfloat16)
    )
    grad_keys = (
        rotate_back(grad_keys, cosine, sine_table).reshape(TOK_DEV, KVW).astype(jnp.bfloat16)
    )
    grad_values = grad_values.reshape(TOK_DEV, KVW).astype(jnp.bfloat16)
    grad_wq = product_left(normed_attn, grad_queries)
    grad_wk = product_left(normed_attn, grad_keys)
    grad_wv = product_left(normed_attn, grad_values)
    grad_normed_attn = (
        product_right(grad_queries, w_q)
        + product_right(grad_keys, w_k)
        + product_right(grad_values, w_v)
    )
    grad_state_norm, grad_gain_attn = norm_back(grad_normed_attn, state, rms_attn, gain_pair[0])
    grad_state = grad_middle + grad_state_norm
    return (
        grad_state,
        (grad_wq, grad_wk, grad_wv, grad_wo, grad_wg, grad_wu, grad_wd),
        jnp.stack([grad_gain_attn, grad_gain_ffn]),
    )


def per_device(
    inputs, seq_lengths, w_query, w_key, w_value, w_out, w_gate, w_up, w_down, norm_gains, cotangent
):
    devices = lax.axis_size("fsdp")
    segment, cosine, sine_table = token_layout(seq_lengths[0])
    flat = flat_shards((w_query, w_key, w_value, w_out, w_gate, w_up, w_down))
    whole = (
        lax.all_gather(flat[0], "fsdp", axis=0, tiled=True),
        lax.all_gather(flat[1], "fsdp", axis=0, tiled=True),
        lax.all_gather(flat[2], "fsdp", axis=0, tiled=True),
        lax.all_gather(flat[3], "fsdp", axis=0, tiled=True),
        lax.all_gather(flat[4], "fsdp", axis=0, tiled=True),
        lax.all_gather(flat[5], "fsdp", axis=0, tiled=True),
        lax.all_gather(flat[6], "fsdp", axis=0, tiled=True),
        lax.all_gather(norm_gains, "fsdp", axis=0, tiled=True),
    )
    weights = [unpack(whole, layer_index, devices) for layer_index in range(LAYERS)]
    gains = whole[7].reshape(LAYERS, 2, D).astype(jnp.float32)
    state = inputs.astype(jnp.float32)
    saved = []
    for layer_index in range(LAYERS):
        state, kept_layer = layer_forward(
            state, weights[layer_index], gains[layer_index], segment, cosine, sine_table
        )
        saved.append(kept_layer)
    outputs = state.astype(jnp.bfloat16)
    whole = (
        lax.all_gather(flat[0], "fsdp", axis=0, tiled=True),
        lax.all_gather(flat[1], "fsdp", axis=0, tiled=True),
        lax.all_gather(flat[2], "fsdp", axis=0, tiled=True),
        lax.all_gather(flat[3], "fsdp", axis=0, tiled=True),
        lax.all_gather(flat[4], "fsdp", axis=0, tiled=True),
        lax.all_gather(flat[5], "fsdp", axis=0, tiled=True),
        lax.all_gather(flat[6], "fsdp", axis=0, tiled=True),
        lax.all_gather(norm_gains, "fsdp", axis=0, tiled=True),
    )
    weights = [unpack(whole, layer_index, devices) for layer_index in range(LAYERS)]
    gains = whole[7].reshape(LAYERS, 2, D).astype(jnp.float32)
    grad_state = cotangent.astype(jnp.float32)
    layer_grads = [None] * LAYERS
    gain_grads = [None] * LAYERS
    shard_grads = [None] * LAYERS
    gain_result = None
    for layer_index in reversed(range(LAYERS)):
        grad_state, layer_grads[layer_index], gain_grads[layer_index] = layer_backward(
            grad_state,
            saved[layer_index],
            weights[layer_index],
            gains[layer_index],
            segment,
            cosine,
            sine_table,
        )
        grad_q, grad_k, grad_v, grad_o, grad_g, grad_u, grad_d = [
            member.reshape(-1) for member in layer_grads[layer_index]
        ]
        if layer_index > 0:
            shard_grads[layer_index] = (
                lax.psum_scatter(grad_q, "fsdp", scatter_dimension=0, tiled=True),
                lax.psum_scatter(grad_k, "fsdp", scatter_dimension=0, tiled=True),
                lax.psum_scatter(grad_v, "fsdp", scatter_dimension=0, tiled=True),
                lax.psum_scatter(grad_o, "fsdp", scatter_dimension=0, tiled=True),
                lax.psum_scatter(grad_g, "fsdp", scatter_dimension=0, tiled=True),
                lax.psum_scatter(grad_u, "fsdp", scatter_dimension=0, tiled=True),
                lax.psum_scatter(grad_d, "fsdp", scatter_dimension=0, tiled=True),
            )
        else:
            gain_total = jnp.stack(gain_grads).reshape(-1)
            summed = (
                lax.psum_scatter(grad_q, "fsdp", scatter_dimension=0, tiled=True),
                lax.psum_scatter(grad_k, "fsdp", scatter_dimension=0, tiled=True),
                lax.psum_scatter(grad_v, "fsdp", scatter_dimension=0, tiled=True),
                lax.psum_scatter(grad_o, "fsdp", scatter_dimension=0, tiled=True),
                lax.psum_scatter(grad_g, "fsdp", scatter_dimension=0, tiled=True),
                lax.psum_scatter(grad_u, "fsdp", scatter_dimension=0, tiled=True),
                lax.psum_scatter(grad_d, "fsdp", scatter_dimension=0, tiled=True),
                lax.psum_scatter(gain_total, "fsdp", scatter_dimension=0, tiled=True),
            )
            shard_grads[0] = summed[:7]
            gain_result = summed[7]
    final = [
        jnp.stack([shard_grads[layer_index][member_index] for layer_index in range(LAYERS)], axis=0)
        for member_index in range(7)
    ]
    return (
        outputs,
        grad_state.astype(jnp.bfloat16),
        final[0],
        final[1],
        final[2],
        final[3],
        final[4],
        final[5],
        final[6],
        gain_result,
    )

def fast_sizes(devices):
    if devices & (devices - 1) or D % devices or FF % devices:
        return None
    rows = D // devices
    pad = -(-rows // 8) * 8
    if devices < 8 or FF // devices != 2 * pad or rows == pad:
        return None
    if LAYERS * 2 * rows > 128:
        return None
    return (rows, pad)


def exchange(value, bit, devices):
    return lax.ppermute(value, "fsdp", [(i, i ^ bit) for i in range(devices)])


def tie(*values):
    return lax.optimization_barrier(values)


def gather_step(held, bit, bits, devices):
    return jnp.concatenate([held, exchange(held, bit, devices)], axis=bits.index(bit))


class Reduction:
    def __init__(self, keep, send, order, bits, devices):
        self.bits, self.devices = bits, devices
        self.shape = (1,) + (2,) * (len(bits) - 1) + (keep.shape[0] * 2 // devices, keep.shape[1])
        self.todo = list(reversed(order))[1:]
        self.total = None
        self.keep = keep.reshape(self.shape)
        self.pending = exchange(send.reshape(self.shape), order[-1], devices)

    def advance(self):
        if self.total is not None:
            return
        total = self.keep.astype(jnp.float32) + self.pending.astype(jnp.float32)
        if not self.todo:
            self.pending = None
            self.total = total.reshape(self.shape[-2:])
            return
        bit = self.todo.pop(0)
        axis = self.bits.index(bit)
        total = total.astype(jnp.bfloat16)
        self.keep = lax.slice_in_dim(total, 0, 1, axis=axis)
        self.pending = exchange(lax.slice_in_dim(total, 1, 2, axis=axis), bit, self.devices)

    def finish(self):
        while self.total is None:
            self.advance()
        return self.total


def advance_under(value, reductions):
    waiting = [item for item in reductions if item.total is None]
    tied = tie(value, *[item.pending for item in waiting])
    for item, pending in zip(waiting, tied[1:]):
        item.pending = pending
        item.advance()
    return tied[0]


PAIR = 2 * HD
ROTATED = (H + KVH) * HD
QUERIES = 256
scale_low = 1.0 / math.sqrt(HD)


def lane_of(shape):
    return lax.broadcasted_iota(jnp.int32, shape, 1)


def attention_kernel(qkv, cosine, sine, bias, rotated, mixed, totals):
    low = jnp.bfloat16
    lane = lane_of((TOK_DEV, PAIR))
    early = (lane % HD) < HD // 2
    for start in range(0, ROTATED, PAIR):
        part = qkv[:, start : start + PAIR]
        turned = jnp.where(
            early, -pltpu.roll(part, PAIR - HD // 2, 1), pltpu.roll(part, HD // 2, 1)
        )
        part = part * cosine[...] + turned * sine[...]
        part = jnp.where(lane + start < D, part * scale_low, part)
        rotated[:, start : start + PAIR] = part.astype(low)
    rotated[:, ROTATED:] = qkv[:, ROTATED:].astype(low)
    for head in range(H):
        group = head // (H // KVH)
        keys = rotated[:, D + group * HD : D + (group + 1) * HD]
        values = rotated[:, ROTATED + group * HD : ROTATED + (group + 1) * HD]
        queries = rotated[:, head * HD : (head + 1) * HD]
        for first in range(0, TOK_DEV, QUERIES):
            last = first + QUERIES
            scores = product_right(keys[:last], queries[first:last]) + bias[:last, first:last]
            largest = jnp.max(scores, axis=0, keepdims=True)
            weights = jnp.exp(scores - largest)
            weight_sum = jnp.sum(weights, axis=0, keepdims=True)
            probs = (weights * (1.0 / weight_sum)).astype(low)
            result = product_left(values[:last], probs)
            mixed[first:last, head * HD : (head + 1) * HD] = result.T.astype(low)
            totals[head : head + 1, first:last] = largest + jnp.log(weight_sum)


def attention(qkv, cosine, sine, bias):
    vmem = pl.BlockSpec(memory_space=pltpu.VMEM)
    return pl.pallas_call(
        attention_kernel,
        out_shape=[
            jax.ShapeDtypeStruct(qkv.shape, jnp.bfloat16),
            jax.ShapeDtypeStruct((TOK_DEV, D), jnp.bfloat16),
            jax.ShapeDtypeStruct((2 * 8, TOK_DEV), jnp.float32),
        ],
        in_specs=[vmem] * 4,
        out_specs=[vmem] * 3,
        name="attention",
    )(qkv, cosine, sine, bias)


def attention_back_kernel(rotated, grad_mixed, totals, cosine, sine, bias, grads, held):
    low = jnp.bfloat16
    for group in range(KVH):
        keys = rotated[:, D + group * HD : D + (group + 1) * HD]
        values = rotated[:, ROTATED + group * HD : ROTATED + (group + 1) * HD]
        blocks = TOK_DEV // QUERIES
        grad_keys = [jnp.zeros((QUERIES, HD), jnp.float32)] * blocks
        grad_values = [jnp.zeros((QUERIES, HD), jnp.float32)] * blocks
        for head in range(group * (H // KVH), (group + 1) * (H // KVH)):
            queries = rotated[:, head * HD : (head + 1) * HD]
            branch = grad_mixed[:, head * HD : (head + 1) * HD]
            for first in range(0, TOK_DEV, QUERIES):
                last = first + QUERIES
                rows = queries[first:last]
                upper = branch[first:last]
                scores = product_right(keys[:last], rows) + bias[:last, first:last]
                probs = jnp.exp(scores - totals[head : head + 1, first:last])
                more_values = product(probs.astype(low), upper)
                grad_probs = product_right(values[:last], upper)
                inner = jnp.sum(probs * grad_probs, axis=0, keepdims=True)
                grad_scores = (probs * (grad_probs - inner)).astype(low)
                more_keys = product(grad_scores, rows)
                held[first:last, head * HD : (head + 1) * HD] = (
                    product_left(grad_scores, keys[:last]) * scale_low
                )
                for i in range(last // QUERIES):
                    part = slice(i * QUERIES, (i + 1) * QUERIES)
                    grad_keys[i] = grad_keys[i] + more_keys[part]
                    grad_values[i] = grad_values[i] + more_values[part]
        for i in range(blocks):
            part = slice(i * QUERIES, (i + 1) * QUERIES)
            held[part, D + group * HD : D + (group + 1) * HD] = grad_keys[i]
            grads[part, ROTATED + group * HD : ROTATED + (group + 1) * HD] = grad_values[
                i
            ].astype(low)
    early = (lane_of((TOK_DEV, PAIR)) % HD) < HD // 2
    for start in range(0, ROTATED, PAIR):
        part = held[:, start : start + PAIR]
        shifted = part * sine[...]
        turned = jnp.where(
            early, pltpu.roll(shifted, PAIR - HD // 2, 1), -pltpu.roll(shifted, HD // 2, 1)
        )
        grads[:, start : start + PAIR] = (part * cosine[...] + turned).astype(low)


def attention_back(rotated, grad_mixed, totals, cosine, sine, bias):
    vmem = pl.BlockSpec(memory_space=pltpu.VMEM)
    return pl.pallas_call(
        attention_back_kernel,
        out_shape=jax.ShapeDtypeStruct(rotated.shape, jnp.bfloat16),
        in_specs=[vmem] * 6,
        out_specs=vmem,
        scratch_shapes=[pltpu.VMEM((TOK_DEV, ROTATED), jnp.float32)],
        name="attention_back",
    )(rotated, grad_mixed, totals, cosine, sine, bias)


def ffn_grads_kernel(owner, normed, gate, upper, hidden, branch, *refs):
    keep_g, send_g, keep_u, send_u, down = refs
    half, pad = keep_g.shape[0], down.shape[1]
    low = jnp.bfloat16
    for source, keep, send in ((gate, keep_g, send_g), (upper, keep_u, send_u)):
        for rows, target in ((0, keep), (half, send)):
            target[:, :FF] = product_left(normed[:, rows : rows + half], source[...]).astype(low)
    down[...] = product_left(hidden[...], branch[...]).reshape(down.shape)
    blocks = half // pad
    for target, even, start in (
        (keep_g, 0, 0),
        (send_g, 0, blocks),
        (keep_u, 1, 0),
        (send_u, 1, blocks),
    ):
        for k in range(0, blocks, 2):
            pair = [down[owner[start + k + i] * 2 + even] for i in range(2)]
            target[k * pad : (k + 2) * pad, FF:] = jnp.concatenate(pair, axis=0).astype(low)


def ffn_grads(owner, normed, gate, upper, hidden, branch):
    half = normed.shape[1] // 2
    blocks = owner.shape[0]
    shape = jax.ShapeDtypeStruct((half, FF + D), jnp.bfloat16)
    vmem = pl.BlockSpec(memory_space=pltpu.VMEM)
    return pl.pallas_call(
        ffn_grads_kernel,
        out_shape=[shape] * 4,
        in_specs=[pl.BlockSpec(memory_space=pltpu.SMEM)] + [vmem] * 5,
        out_specs=[vmem] * 4,
        scratch_shapes=[pltpu.VMEM((2 * blocks, FF // blocks // 2, D), jnp.float32)],
        name="ffn_grads",
    )(owner, normed, gate, upper, hidden, branch)


def attn_grads_kernel(normed, grad_qkv, attended, branch, extra, keep, send):
    half = keep.shape[0]
    low = jnp.bfloat16
    wide = grad_qkv.shape[1]
    share = extra.shape[1]
    for rows, target in ((0, keep), (half, send)):
        grads = product_left(normed[:, rows : rows + half], grad_qkv[...])
        target[:, share:wide] = grads[:, share:].astype(low)
        target[:, :share] = (grads[:, :share] + extra[rows : rows + half, :]).astype(low)
        target[:, wide:] = product_left(attended[:, rows : rows + half], branch[...]).astype(low)


def attn_grads(normed, grad_qkv, attended, branch, extra):
    half = normed.shape[1] // 2
    shape = jax.ShapeDtypeStruct((half, grad_qkv.shape[1] + D), jnp.bfloat16)
    vmem = pl.BlockSpec(memory_space=pltpu.VMEM)
    return pl.pallas_call(
        attn_grads_kernel,
        out_shape=[shape] * 2,
        in_specs=[vmem] * 5,
        out_specs=[vmem] * 2,
        name="attn_grads",
    )(normed, grad_qkv, attended, branch, extra)


def fast_device(
    inputs, seq_lengths, w_query, w_key, w_value, w_out, w_gate, w_up, w_down, norm_gains, cotangent
):
    devices = lax.axis_size("fsdp")
    rows, pad = fast_sizes(devices)
    low = jnp.bfloat16
    segment, cosine, sine_table = token_layout(seq_lengths[0])
    cosine = jnp.concatenate([cosine[:, 0]] * 2, axis=-1)
    sine_table = jnp.concatenate([sine_table[:, 0]] * 2, axis=-1)
    token = jnp.arange(TOK_DEV, dtype=jnp.int32)
    allowed = (segment[:, None] == segment[None, :]) & (token[:, None] <= token[None, :])
    bias = jnp.where(allowed, 0.0, masked_score).astype(jnp.float32)
    me = lax.axis_index("fsdp")

    count = devices.bit_length() - 1
    bits = [1] + [1 << i for i in range(count - 1, 0, -1)]
    rest = bits[1:]
    first, others = rest[:1], rest[1:]

    def turned(shift):
        shift = shift % max(len(others), 1)
        return first + others[shift:] + others[:shift] + [1]

    orders = (turned(1), turned(2), turned(0))
    orders = tuple([o[:1] + o[1:-1][::-1] + o[-1:] for o in orders])

    block = jnp.arange(devices, dtype=jnp.int32)
    half = devices // 2
    owner = me ^ (((block % half) << 1) | (block // half))
    other = me ^ block
    place = (other >> 1) + (other & 1) * half

    column = jnp.arange(devices * pad, dtype=jnp.int32)
    inside = column % pad
    feature = jnp.where(inside < rows, jnp.repeat(owner, pad) * rows + inside, -1)
    spread = (jnp.arange(D, dtype=jnp.int32)[:, None] == feature[None, :]).astype(low)

    def spread_out(value):
        return jnp.dot(value, spread, preferred_element_type=jnp.float32).astype(low)

    def bring_back(value):
        return product_right(value.astype(low), spread)

    def packed(layer):
        def cut(member, width):
            return member[layer].reshape(rows, width)

        folded = w_down[layer].reshape(2, pad, D)

        def padded(members):
            return jnp.pad(jnp.concatenate(members, axis=1), ((0, pad - rows), (0, 0)))

        attn = padded([cut(w_query, D), cut(w_key, KVW), cut(w_value, KVW), cut(w_out, D)])
        if layer == 0:
            share = norm_gains.shape[0]
            attn = attn + jnp.pad(
                norm_gains[None, :], ((rows, pad - rows - 1), (0, attn.shape[1] - share))
            )
        gate = jnp.concatenate([padded([cut(w_gate, FF)]), folded[0]], axis=1)
        upper = jnp.concatenate([padded([cut(w_up, FF)]), folded[1]], axis=1)
        return (attn, gate, upper)

    slabs = [
        [slab.reshape((1,) * count + slab.shape) for slab in packed(layer)]
        for layer in range(LAYERS)
    ]
    share = norm_gains.shape[0]
    wide = D + 2 * KVW
    level = [0] * LAYERS

    def gather_more(layer, steps):
        for _ in range(steps):
            slabs[layer] = [
                gather_step(slabs[layer][i], orders[i][level[layer]], bits, devices)
                for i in range(3)
            ]
            level[layer] += 1

    def gather_tied(layer, steps, value):
        tied = tie(value, *slabs[layer])
        slabs[layer] = list(tied[1:])
        gather_more(layer, min(steps, count - level[layer]))
        return tied[0]

    gather_more(0, count - 2)
    gather_more(1, count - 2)
    gather_more(0, 1)
    tied = tie(*slabs[0], *slabs[1])
    slabs[0], slabs[1] = list(tied[:3]), list(tied[3:])
    gather_more(0, 1)
    gather_more(1, 1)

    def unpacked(layer):
        attn, gate, upper = [member.reshape(devices * pad, -1) for member in slabs[layer]]
        folds = [member[:, FF:].reshape(devices, pad, D) for member in (gate, upper)]
        down = jnp.take(jnp.stack(folds, axis=1), place, axis=0).reshape(FF, D)
        return (attn[:, :wide], attn[:, wide:], gate[:, :FF], upper[:, :FF], down)

    weights = [unpacked(0)] + [None] * (LAYERS - 1)
    gains = jnp.take(slabs[0][0].reshape(devices, pad, -1)[:, rows, :share], place, axis=0)
    gains = gains.reshape(LAYERS, 2, D).astype(jnp.float32)

    def forward(state, layer):
        w_qkv, w_o, w_g, w_u, w_d = weights[layer]
        gain_pair = gains[layer]
        rms_attn = lax.rsqrt(jnp.mean(state * state, axis=-1, keepdims=True) + epsilon)
        normed_attn = spread_out((state * rms_attn * gain_pair[0]).astype(low))
        qkv = product(normed_attn, w_qkv)
        rotated, mixed, totals = attention(qkv, cosine, sine_table, bias)
        attended = spread_out(mixed)
        middle = state + product(attended, w_o)
        rms_ffn = lax.rsqrt(jnp.mean(middle * middle, axis=-1, keepdims=True) + epsilon)
        normed_ffn = spread_out((middle * rms_ffn * gain_pair[1]).astype(low))
        gate = product(normed_ffn, w_g)
        up_part = product(normed_ffn, w_u)
        hidden = (jax.nn.silu(gate) * up_part).astype(low)
        if layer == 0:
            hidden = gather_tied(1, 1, hidden)
        result = middle + product(hidden, w_d)
        saved = (
            state,
            rms_attn,
            normed_attn,
            rotated,
            totals,
            attended,
            middle,
            rms_ffn,
            normed_ffn,
            gate,
            up_part,
            hidden,
        )
        return (result, saved)

    def backward(grad_result, saved, layer):
        w_qkv, w_o, w_g, w_u, w_d = weights[layer]
        gain_pair = gains[layer]
        (
            state,
            rms_attn,
            normed_attn,
            rotated,
            totals,
            attended,
            middle,
            rms_ffn,
            normed_ffn,
            gate,
            up_part,
            hidden,
        ) = saved
        grad_branch = grad_result.astype(low)
        grad_hidden = product_right(grad_branch, w_d)
        sigmoid_gate = jax.nn.sigmoid(gate)
        grad_gate = (
            grad_hidden * up_part * sigmoid_gate * (1.0 + gate * (1.0 - sigmoid_gate))
        ).astype(low)
        grad_upper = (grad_hidden * gate * sigmoid_gate).astype(low)
        keep_g, send_g, keep_u, send_u = ffn_grads(
            owner, normed_ffn, grad_gate, grad_upper, hidden, grad_branch
        )
        grad_gate = advance_under(grad_gate, active)
        active.append(Reduction(keep_g, send_g, orders[1], bits, devices))
        active.append(Reduction(keep_u, send_u, orders[2], bits, devices))
        grad_normed_ffn = bring_back(product_right(grad_gate, w_g) + product_right(grad_upper, w_u))
        grad_mid_norm, grad_gain_ffn = norm_back(grad_normed_ffn, middle, rms_ffn, gain_pair[1])
        grad_middle = grad_result + grad_mid_norm
        grad_attn_branch = grad_middle.astype(low)
        grad_mixed = bring_back(product_right(grad_attn_branch, w_o)).astype(low)
        grad_mixed = advance_under(grad_mixed, active)
        grad_qkv = attention_back(rotated, grad_mixed, totals, cosine, sine_table, bias)
        grad_qkv = advance_under(grad_qkv, active)
        grad_normed_attn = bring_back(product_right(grad_qkv, w_qkv))
        grad_state_norm, grad_gain_attn = norm_back(grad_normed_attn, state, rms_attn, gain_pair[0])
        grad_state = grad_middle + grad_state_norm
        gain_grads[layer] = jnp.stack([grad_gain_attn, grad_gain_ffn])
        extra = jnp.zeros((devices * pad, 128), jnp.float32)
        if layer == 0:
            total = jnp.take(jnp.stack(gain_grads).reshape(devices, share), owner, axis=0)
            total = jnp.pad(total[:, None, :], ((0, 0), (rows, pad - rows - 1), (0, 128 - share)))
            extra = total.reshape(extra.shape)
        keep, send = attn_grads(normed_attn, grad_qkv, attended, grad_attn_branch, extra)
        active.append(Reduction(keep, send, orders[0], bits, devices))
        return grad_state

    state = inputs.astype(jnp.float32)
    kept = []
    for layer in range(LAYERS):
        if layer > 0:
            weights[layer] = unpacked(layer)
        state, saved = forward(state, layer)
        kept.append(saved)
    outputs = state.astype(low)
    grad_state = cotangent.astype(jnp.float32)
    gain_grads = [None] * LAYERS
    active = []
    for layer in reversed(range(LAYERS)):
        grad_state = backward(grad_state, kept[layer], layer)
    sums = [item.finish() for item in active]
    shards = [sums[3 * (LAYERS - 1 - layer) :][:3] for layer in range(LAYERS)]

    gain_result = shards[0][2][rows, :share]
    results = []
    bounds = (0, D, D + KVW, wide, wide + D)
    for index in range(4):
        results.append([part[2][:rows, bounds[index] : bounds[index + 1]] for part in shards])
    results.append([part[0][:rows, :FF] for part in shards])
    results.append([part[1][:rows, :FF] for part in shards])
    results.append([jnp.stack([part[0][:, FF:], part[1][:, FF:]]) for part in shards])
    final = [jnp.stack([member.reshape(-1) for member in pair], axis=0) for pair in results]
    return (
        outputs,
        grad_state.astype(low),
        final[0],
        final[1],
        final[2],
        final[3],
        final[4],
        final[5],
        final[6],
        gain_result,
    )


def solution(mesh):
    placed = (
        P("fsdp", None),
        P("fsdp", None),
        P(None, "fsdp"),
        P(None, "fsdp"),
        P(None, "fsdp"),
        P(None, "fsdp"),
        P(None, "fsdp"),
        P(None, "fsdp"),
        P(None, "fsdp"),
        P("fsdp"),
        P("fsdp", None),
    )
    body = per_device if fast_sizes(mesh.shape["fsdp"]) is None else fast_device
    return jax.shard_map(
        body,
        mesh=mesh,
        in_specs=placed,
        out_specs=(
            P("fsdp", None),
            P("fsdp", None),
            P(None, "fsdp"),
            P(None, "fsdp"),
            P(None, "fsdp"),
            P(None, "fsdp"),
            P(None, "fsdp"),
            P(None, "fsdp"),
            P(None, "fsdp"),
            P("fsdp"),
        ),
        check_vma=False,
    )
```
